512 devices in a mesh: pipe: 32 (over x, z), expert: 16 (over y, core).
Axes of the slice: x: 4, y: 8, z: 8, core: 2. Of those that a mesh axis runs over, the one named last changes fastest.
Arguments:
- upstream: bfloat16 [32, 1024, 7168], P('pipe', None, 'expert'), may hold values from -6 to 6
- shared_down: bfloat16 [32, 1024, 7168], P('pipe', None, 'expert'), may hold values from -0.0625 to 0.0625
- shared_gate: bfloat16 [32, 7168, 1024], P('pipe', 'expert'), may hold values from -0.1875 to 0.1875
- shared_up: bfloat16 [32, 7168, 1024], P('pipe', 'expert'), may hold values from -0.1875 to 0.1875
- router_weight: bfloat16 [32, 7168, 256], P('pipe', 'expert'), may hold values from -2 to 2
- gate_pre: bfloat16 [32, 1024, 1024], P('pipe', 'expert'), may hold values from -6 to 6
- up_pre: bfloat16 [32, 1024, 1024], P('pipe', 'expert'), may hold values from -6 to 6
- gate_grad: float32 [32, 1024, 8], P('pipe'), may hold values from -6 to 6
- gate_scores: float32 [32, 1024, 8], P('pipe'), may hold values from 0.05 to 0.95
- expert_ids: int32 [32, 1024, 8], P('pipe'), may hold values from 0 to 255, all different within a row
Outputs:
- down_grad: bfloat16 [32, 1024, 7168], P('pipe', None, 'expert')
The draws below stay inside these ranges and needn't reach their ends.
Inputs may be any that keep to these rules, and one draw needn't show every extreme that they name: `expert_ids`: each token names 8 different experts.
All inputs are finite; a program needn't handle non-finite values.
Results may differ from the reference program's by a relative error of at most 0.02.
Values may be sent and summed in bfloat16 or wider, within the bound.
A program may use at most 64 MiB of HBM per device.

```python
import jax
import jax.numpy as jnp
from jax import lax

D = 7168
NEXP = 256
TOP = 8
HID = 1024
TOK = 1024
N_PIPE = 32
N_EXPERT = 16


def steps_of(own_key, dims, shards, low, high):
    def one(dim, parts):
        steps = jax.random.uniform(jax.random.fold_in(jax.random.fold_in(own_key, 6), dim), (parts,), jnp.float32, low / len(shards), high / len(shards))
        return jnp.repeat(jnp.exp(steps), dims[dim] // parts).reshape((-1,) + (1,) * (len(dims) - dim - 1))

    level = one(*shards[0])
    for cut in shards[1:]:
        level = level * one(*cut)
    return level


def different_ones(rng, rows, amount, top, lift):
    ranking = jax.random.permutation(jax.random.fold_in(rng, 1), amount)
    boost = ranking
    for power in range(3):
        boost = boost * boost // amount
    boost = boost * lift // amount
    chance = jax.random.randint(jax.random.fold_in(rng, 2), (rows, amount), 0, 4096) + boost
    holders = jax.random.permutation(jax.random.fold_in(rng, 3), rows)[jnp.arange(amount) % rows]
    chance = jnp.where(jnp.arange(rows)[:, None] == holders[None, :], 1 << 14, chance)
    score = chance * amount + jnp.arange(amount)
    return lax.top_k(score.astype(jnp.int32), top)[1].astype(jnp.int32)


def noise(key, dims, scale, most, shards=(), kind=jnp.bfloat16):
    loudness = steps_of(key, dims, shards, -0.22, 0.18) if shards else 1.0
    values = jax.random.normal(key, dims, jnp.float32) * scale * loudness
    return jnp.minimum(jnp.maximum(values, -most), most).astype(kind)


def setup_inputs(seed: int = 0) -> dict:
    keys = jax.random.split(jax.random.key(seed), 11)
    return {
        "upstream": noise(keys[0], (N_PIPE, TOK, D), 1.0, 6.0, ((0, 32), (2, 16))),
        "shared_down": noise(keys[1], (N_PIPE, HID, D), D ** -0.5, 0.0625, ((0, 32), (2, 16))),
        "shared_gate": noise(keys[2], (N_PIPE, D, HID), HID ** -0.5, 0.1875, ((0, 32), (1, 16))),
        "shared_up": noise(keys[3], (N_PIPE, D, HID), HID ** -0.5, 0.1875, ((0, 32), (1, 16))),
        "router_weight": noise(keys[4], (N_PIPE, D, NEXP), TOP ** -0.5, 2.0, ((0, 32), (1, 16))),
        "gate_pre": noise(keys[5], (N_PIPE, TOK, HID), 1.0, 6.0, ((0, 32), (1, 16))),
        "up_pre": noise(keys[6], (N_PIPE, TOK, HID), 1.0, 6.0, ((0, 32), (1, 16))),
        "gate_grad": noise(keys[7], (N_PIPE, TOK, TOP), 1.0, 6.0, ((0, 32),), jnp.float32),
        "gate_scores": jnp.clip(0.05 + 0.9 * jax.random.uniform(keys[8], (N_PIPE, TOK, TOP), jnp.float32) ** steps_of(keys[8], (N_PIPE, TOK, TOP), ((0, 32),), -0.2, 0.2), 0.05, 0.95),
        "expert_ids": different_ones(keys[9], N_PIPE * TOK, NEXP, TOP, 512).reshape((N_PIPE, TOK, TOP)),
    }


def section_backward(params):
    incoming, w_down, w_gate, w_up, w_router, pre_gate, pre_up, grad_gate, scores, chosen = params
    width = incoming.shape[1] // N_EXPERT
    hidden_grad = jnp.zeros((incoming.shape[0], w_down.shape[0]), jnp.float32)
    for block in range(N_EXPERT):
        part = jnp.dot(incoming[:, block * width:(block + 1) * width], w_down[:, block * width:(block + 1) * width].T, preferred_element_type=jnp.float32)
        hidden_grad = hidden_grad + part.astype(jnp.bfloat16).astype(jnp.float32)
    act_a = pre_gate.astype(jnp.float32)
    act_b = pre_up.astype(jnp.float32)
    sigma = jax.nn.sigmoid(act_a)
    gate_part = (hidden_grad * act_b * sigma * (1.0 + act_a * (1.0 - sigma))).astype(jnp.bfloat16)
    up_part = (hidden_grad * act_a * sigma).astype(jnp.bfloat16)
    total = jnp.sum(scores, axis=-1, keepdims=True)
    mixed = jnp.sum(grad_gate * scores, axis=-1, keepdims=True)
    logit_grad = 2.5 * (grad_gate - mixed / total) / total * scores * (1.0 - scores)
    columns = jnp.arange(NEXP, dtype=jnp.int32)
    dense = jnp.zeros((grad_gate.shape[0], NEXP), jnp.float32)
    for slot in range(TOP):
        dense = dense + jnp.where(chosen[:, slot:slot + 1] == columns[None, :], logit_grad[:, slot:slot + 1], 0.0)
    dense_grad = dense.astype(jnp.bfloat16)
    result = jnp.dot(gate_part, w_gate.T, preferred_element_type=jnp.float32)
    result = result + jnp.dot(up_part, w_up.T, preferred_element_type=jnp.float32)
    result = result + jnp.dot(dense_grad, w_router.T, preferred_element_type=jnp.float32)
    return result.astype(jnp.bfloat16)


def reference(upstream, shared_down, shared_gate, shared_up, router_weight, gate_pre, up_pre, gate_grad, gate_scores, expert_ids):
    def ahead(arr, steps):
        return jnp.roll(arr, -steps, axis=0)
    params = (ahead(upstream, 2), ahead(shared_down, 1), ahead(shared_gate, 1), ahead(shared_up, 1),
              ahead(router_weight, 1), ahead(gate_pre, 1), ahead(up_pre, 1), ahead(gate_grad, 1),
              ahead(gate_scores, 1), ahead(expert_ids, 1))
    return lax.map(section_backward, params)
```

```python
import functools

import jax
import jax.numpy as jnp
from jax import lax
from jax.experimental import pallas as pl
from jax.experimental.pallas import tpu as pltpu
from jax.sharding import PartitionSpec as P

MESH = pl.DeviceIdType.MESH
F32 = jnp.float32
BF16 = jnp.bfloat16
NEAR = (4, 2, -2, 0)
FAR = (3, -3, 1, -1)
ARRIVAL = ((0, 0), (1, 0), (1, 1), (0, 1), (0, 2), (1, 2), (1, 3), (0, 3))


def kernel(
    n_pipe, n_chip,
    up_ref, dn_ref, wg_ref, wu_ref, wr_ref, pa_ref, pb_ref, gg_ref, sc_ref, id_ref,
    out_ref,
    up, dn, wg, wu, wr, pa, pb, gg, sc, ids, c1, c2, pf, rbuf, sbuf, gbuf, rterm, obuf,
    loc_sem, a_send, a_recv, w_send, w_recv, rs_send, rs_recv, ag_send, ag_recv, d_send, d_recv,
):
    feat = up_ref.shape[0]
    tile = pa_ref.shape[0] * 2
    hid = pa_ref.shape[1]
    half = hid // 2
    p = lax.axis_index("pipe")
    e = lax.axis_index("expert")
    y, c = e // 2, e % 2
    role = lax.rem(c + y, 2)
    before = lax.rem(p + n_pipe - 1, n_pipe)
    after = lax.rem(p + 1, n_pipe)
    partner = (p, 2 * y + 1 - c)
    plus = (p, 2 * lax.rem(y + 1, n_chip) + c)
    minus = (p, 2 * lax.rem(y + n_chip - 1, n_chip) + c)
    near = role == 0
    far = role == 1

    def remote(src, dst, send, recv, device):
        return pltpu.make_async_remote_copy(
            src_ref=src, dst_ref=dst, send_sem=send, recv_sem=recv, device_id=device, device_id_type=MESH
        )

    def arrived(dst, recv):
        remote(dst, dst, recv, recv, partner).wait_recv()

    def sent(src, send):
        remote(src, src, send, send, partner).wait_send()

    barrier = pltpu.get_barrier_semaphore()
    for device in ((after, 2 * y), (after, 2 * y + 1), partner, plus, minus):
        pl.semaphore_signal(barrier, inc=1, device_id=device, device_id_type=MESH)

    mine = pl.ds(pl.multiple_of(c * feat, feat), feat)
    mine_rows = pl.ds(pl.multiple_of(c * (tile // 2), tile // 2), tile // 2)
    wide = ((dn_ref, dn, mine), (wr_ref, wr, mine), (pa_ref, pa, mine_rows), (pb_ref, pb, mine_rows),
            (wg_ref, wg, mine), (wu_ref, wu, mine))
    local = [pltpu.make_async_copy(s, d, loc_sem.at[i]) for i, (s, d) in enumerate(((gg_ref, gg), (sc_ref, sc), (id_ref, ids)))]
    local += [pltpu.make_async_copy(s, d.at[rows], loc_sem.at[3 + i]) for i, (s, d, rows) in enumerate(wide)]
    for copy in local:
        copy.start()

    pl.semaphore_wait(barrier, 5)

    def lanes(distance):
        return pl.ds(pl.multiple_of(lax.rem(y + n_chip + distance, n_chip) * tile, tile), tile)

    incoming = []
    for i, (r, s) in enumerate(ARRIVAL):
        device = (before, 2 * y + lax.rem(y + r, 2))
        copy = remote(up_ref.at[:, lanes((NEAR, FAR)[r][s])], up.at[s, mine], a_send.at[i], a_recv.at[s, c], device)
        copy.start()
        incoming.append(copy)
    exchange = [remote(s, d.at[rows], w_send.at[i], w_recv.at[i], partner) for i, (s, d, rows) in enumerate(wide)]
    for copy in exchange:
        copy.start()

    theirs = pl.ds(pl.multiple_of((1 - c) * feat, feat), feat)
    theirs_rows = pl.ds(pl.multiple_of((1 - c) * (tile // 2), tile // 2), tile // 2)

    def have(i):
        rows = theirs_rows if i in (2, 3) else theirs
        local[3 + i].wait()
        arrived(wide[i][1].at[rows], w_recv.at[i])

    def tile_lanes(s):
        distance = jnp.where(near, NEAR[s], FAR[s])
        return pl.ds(pl.multiple_of(lax.rem(y + n_chip + distance, n_chip) * tile, tile), tile)

    for i in range(3):
        local[i].wait()
    have(1)
    for s in range(4):
        where = tile_lanes(s)
        grad, score, chosen = gg[:, where], sc[:, where], ids[:, where]
        total = jnp.sum(score, axis=0, keepdims=True)
        mixed = jnp.sum(grad * score, axis=0, keepdims=True)
        logit = 2.5 * (grad - mixed / total) / total * score * (1.0 - score)
        n_experts = wr.shape[1]
        rows = lax.broadcasted_iota(jnp.int32, (n_experts, tile), 0)
        dense = jnp.zeros((n_experts, tile), F32)
        for k in range(grad.shape[0]):
            dense = dense + jnp.where(chosen[k : k + 1] == rows, logit[k : k + 1], 0.0)
        rterm[s] = jnp.dot(wr[...], dense.astype(BF16), preferred_element_type=F32)

    have(2)
    have(3)

    @pl.when(near)
    def _():
        a, b = pa[...].astype(F32), pb[...].astype(F32)
        sigma = 1.0 / (1.0 + jnp.exp(-a))
        c1[...] = b * sigma * (1.0 + a * (1.0 - sigma))
        c2[...] = a * sigma

    have(0)

    def rs_copy(src, slot, device, send, cols=slice(None)):
        return remote(src.at[:, cols], rbuf.at[slot, :, cols], rs_send.at[send], rs_recv.at[slot], device)

    low, high = pl.ds(0, half), pl.ds(half, half)
    for s in range(4):
        for other in range(2):
            rows = pl.ds(other * feat, feat)
            arrived(up.at[s, rows], a_recv.at[s, other])
        pf[...] = lax.dot_general(up[s], dn[...], (((0,), (0,)), ((), ())), preferred_element_type=F32)

        @pl.when(near)
        def _(s=s):
            if s == 0:
                sbuf[0] = pf[...].astype(BF16)
                rs_copy(sbuf.at[0], 0, plus, 0, low).start()
                rs_copy(sbuf.at[0], 1, minus, 3, high).start()
            elif s < 3:
                arrived(rbuf.at[s - 1], rs_recv.at[s - 1])
                sbuf[s] = (pf[...] + rbuf[s - 1].astype(F32)).astype(BF16)
                rs_copy(sbuf.at[s], s + 1, (plus, minus)[s - 1], s).start()
            else:
                arrived(rbuf.at[2], rs_recv.at[2])
                arrived(rbuf.at[3], rs_recv.at[3])
                hidden = pf[...] + rbuf[2].astype(F32) + rbuf[3].astype(F32)
                gbuf[3, :, :hid] = (hidden * c1[...]).astype(BF16)
                gbuf[3, :, hid:] = (hidden * c2[...]).astype(BF16)

        @pl.when(far)
        def _(s=s):
            if s < 2:
                cols = (low, high)[s]
                arrived(rbuf.at[s, :, cols], rs_recv.at[s])
                if s == 0:
                    sbuf[s, :, :half] = (pf[:, :half] + rbuf[s, :, :half].astype(F32)).astype(BF16)
                    sbuf[s, :, half:] = pf[:, half:].astype(BF16)
                else:
                    sbuf[s, :, :half] = pf[:, :half].astype(BF16)
                    sbuf[s, :, half:] = (pf[:, half:] + rbuf[s, :, half:].astype(F32)).astype(BF16)
            else:
                arrived(rbuf.at[s], rs_recv.at[s])
                sbuf[s] = (pf[...] + rbuf[s].astype(F32)).astype(BF16)
            rs_copy(sbuf.at[s], s, (plus, minus)[s % 2], s).start()

    def ag_copy(here, there, device, send, recv, cols=slice(None)):
        return remote(gbuf.at[here, :, cols], gbuf.at[there, :, cols], ag_send.at[send], ag_recv.at[recv], device)

    gate_cols, up_cols = pl.ds(0, hid), pl.ds(hid, hid)

    have(4)
    have(5)

    @pl.when(near)
    def _():
        ag_copy(3, 3, plus, 0, 3).start()
        ag_copy(3, 2, minus, 1, 2).start()

    for s in (3, 2, 1, 0):

        @pl.when(near)
        def _(s=s):
            if s == 2:
                arrived(gbuf.at[2], ag_recv.at[2])
                ag_copy(2, 1, plus, 2, 1).start()
                arrived(gbuf.at[1], ag_recv.at[1])
                ag_copy(1, 0, minus, 3, 0).start()
            if s == 0:
                arrived(gbuf.at[0, :, gate_cols], ag_recv.at[0])
                arrived(gbuf.at[0, :, up_cols], ag_recv.at[4])

        @pl.when(far)
        def _(s=s):
            if s == 3:
                arrived(gbuf.at[3], ag_recv.at[3])
                ag_copy(3, 2, plus, 0, 2).start()
                arrived(gbuf.at[2], ag_recv.at[2])
                ag_copy(2, 1, minus, 1, 1).start()
            if s == 1:
                arrived(gbuf.at[1], ag_recv.at[1])
                ag_copy(1, 0, plus, 2, 0, gate_cols).start()
                arrived(gbuf.at[0], ag_recv.at[0])
                ag_copy(0, 0, minus, 3, 4, up_cols).start()

        nt = (((1,), (1,)), ((), ()))
        for other in range(2):
            rows = pl.ds(other * feat, feat)
            result = (
                lax.dot_general(wg[rows], gbuf[s, :, :hid], nt, preferred_element_type=F32)
                + lax.dot_general(wu[rows], gbuf[s, :, hid:], nt, preferred_element_type=F32)
                + rterm[s, rows]
            )
            obuf[s, rows] = result.astype(BF16)
            remote(
                obuf.at[s, rows], out_ref.at[:, tile_lanes(s)], d_send.at[s, other], d_recv.at[s, role],
                (before, 2 * y + other),
            ).start()

    for copy in incoming:
        copy.wait_send()
    for copy in exchange:
        copy.wait_send()

    @pl.when(near)
    def _():
        sent(sbuf.at[0, :, low], rs_send.at[0])
        sent(sbuf.at[0, :, high], rs_send.at[3])
        for s in (1, 2):
            sent(sbuf.at[s], rs_send.at[s])
        for s, send in ((3, 0), (3, 1), (2, 2), (1, 3)):
            sent(gbuf.at[s], ag_send.at[send])

    @pl.when(far)
    def _():
        for s in range(4):
            sent(sbuf.at[s], rs_send.at[s])
        sent(gbuf.at[3], ag_send.at[0])
        sent(gbuf.at[2], ag_send.at[1])
        sent(gbuf.at[1, :, gate_cols], ag_send.at[2])
        sent(gbuf.at[0, :, up_cols], ag_send.at[3])

    for s in range(4):
        for other in range(2):
            sent(obuf.at[s, pl.ds(other * feat, feat)], d_send.at[s, other])
            arrived(out_ref.at[:, pl.ds(0, tile)], d_recv.at[s, other])


def shards(upstream, shared_down, shared_gate, shared_up, router_weight, gate_pre, up_pre, gate_grad, gate_scores, expert_ids):
    n_pipe = lax.axis_size("pipe")
    n_chip = lax.axis_size("expert") // 2
    _, tokens, feat = upstream.shape
    rows, hid = gate_pre.shape[1:]
    tile = 2 * rows
    n_experts = router_weight.shape[2]
    top = gate_grad.shape[2]
    args = (
        upstream[0].T, shared_down[0].T, shared_gate[0], shared_up[0], router_weight[0], gate_pre[0], up_pre[0],
        gate_grad[0].T, gate_scores[0].T, expert_ids[0].T,
    )
    vm = pltpu.VMEM
    dma = pltpu.SemaphoreType.DMA
    out = pl.pallas_call(
        functools.partial(kernel, n_pipe, n_chip),
        out_shape=jax.ShapeDtypeStruct((feat, tokens), BF16),
        in_specs=[pl.BlockSpec(memory_space=pl.ANY)] * len(args),
        out_specs=pl.BlockSpec(memory_space=pl.ANY),
        scratch_shapes=[
            vm((4, 2 * feat, tile), BF16),
            vm((2 * feat, hid), BF16),
            vm((2 * feat, hid), BF16),
            vm((2 * feat, hid), BF16),
            vm((2 * feat, n_experts), BF16),
            vm((tile, hid), BF16),
            vm((tile, hid), BF16),
            vm((top, tokens), F32),
            vm((top, tokens), F32),
            vm((top, tokens), jnp.int32),
            vm((tile, hid), F32),
            vm((tile, hid), F32),
            vm((tile, hid), F32),
            vm((4, tile, hid), BF16),
            vm((4, tile, hid), BF16),
            vm((4, tile, 2 * hid), BF16),
            vm((4, 2 * feat, tile), F32),
            vm((4, 2 * feat, tile), BF16),
            dma((9,)), dma((8,)), dma((4, 2)), dma((6,)), dma((6,)),
            dma((4,)), dma((4,)), dma((4,)), dma((5,)), dma((4, 2)), dma((4, 2)),
        ],
        compiler_params=pltpu.CompilerParams(collective_id=0, has_side_effects=True, vmem_limit_bytes=67043328),
    )(*args)
    return out.T[None]


def solution(mesh):
    in_specs = (
        P("pipe", None, "expert"),
        P("pipe", None, "expert"),
        P("pipe", "expert", None),
        P("pipe", "expert", None),
        P("pipe", "expert", None),
        P("pipe", "expert", None),
        P("pipe", "expert", None),
        P("pipe", None, None),
        P("pipe", None, None),
        P("pipe", None, None),
    )
    out_specs = P("pipe", None, "expert")
    return jax.shard_map(shards, mesh=mesh, in_specs=in_specs, out_specs=out_specs, check_vma=False)
```

```python
import functools

import jax
import jax.numpy as jnp
from jax import lax
from jax.experimental import pallas as pl
from jax.experimental.pallas import tpu as pltpu
from jax.sharding import PartitionSpec as P

MESH = pl.DeviceIdType.MESH
F32 = jnp.float32
BF16 = jnp.bfloat16
NEAR = (4, 2, -2, 0)
FAR = (3, -3, 1, -1)
PARTS = 4
LEAVING = tuple(k for i in range(PARTS // 2) for k in (i, PARTS // 2 + i))


def kernel(
    n_pipe, n_chip,
    up_ref, dn_ref, wg_ref, wu_ref, wr_ref, pa_ref, pb_ref, gg_ref, sc_ref, id_ref,
    out_ref,
    up, dn, wg, wu, wr, pa, pb, gg, sc, ids, c1, c2, pf, rbuf, sbuf, gbuf, rterm, obuf,
    loc_sem, a_send, a_recv, w_send, w_recv, rs_send, rs_recv, ag_send, ag_recv, d_send, d_recv,
):
    feat = up_ref.shape[0]
    tile = pa_ref.shape[0] * 2
    hid = pa_ref.shape[1]
    p = lax.axis_index("pipe")
    e = lax.axis_index("expert")
    y, c = e // 2, e % 2
    role = lax.rem(c + y, 2)
    before = lax.rem(p + n_pipe - 1, n_pipe)
    after = lax.rem(p + 1, n_pipe)
    partner = (p, 2 * y + 1 - c)
    plus = (p, 2 * lax.rem(y + 1, n_chip) + c)
    minus = (p, 2 * lax.rem(y + n_chip - 1, n_chip) + c)
    near = role == 0
    far = role == 1

    def remote(src, dst, send, recv, device):
        return pltpu.make_async_remote_copy(
            src_ref=src, dst_ref=dst, send_sem=send, recv_sem=recv, device_id=device, device_id_type=MESH
        )

    def arrived(dst, recv):
        remote(dst, dst, recv, recv, partner).wait_recv()

    def sent(src, send):
        remote(src, src, send, send, partner).wait_send()

    barrier = pltpu.get_barrier_semaphore()
    for device in ((after, 2 * y), (after, 2 * y + 1), partner, plus, minus):
        pl.semaphore_signal(barrier, inc=1, device_id=device, device_id_type=MESH)

    mine = pl.ds(pl.multiple_of(c * feat, feat), feat)
    mine_rows = pl.ds(pl.multiple_of(c * (tile // 2), tile // 2), tile // 2)
    wide = ((dn_ref, dn, mine), (wr_ref, wr, mine), (pa_ref, pa, mine_rows), (pb_ref, pb, mine_rows),
            (wg_ref, wg, mine), (wu_ref, wu, mine))
    local = [pltpu.make_async_copy(s, d, loc_sem.at[i]) for i, (s, d) in enumerate(((gg_ref, gg), (sc_ref, sc), (id_ref, ids)))]
    local += [pltpu.make_async_copy(s, d.at[rows], loc_sem.at[3 + i]) for i, (s, d, rows) in enumerate(wide)]
    for copy in local:
        copy.start()

    pl.semaphore_wait(barrier, 5)

    def lanes(distance):
        return pl.ds(pl.multiple_of(lax.rem(y + n_chip + distance, n_chip) * tile, tile), tile)

    incoming = []
    for i in range(8):
        target, slot = i % 2, i // 2
        distance = jnp.where(lax.rem(target + y, 2) == 0, NEAR[slot], FAR[slot])
        copy = remote(
            up_ref.at[:, lanes(distance)], up.at[slot, mine], a_send.at[i], a_recv.at[slot, c], (before, 2 * y + target)
        )
        copy.start()
        incoming.append(copy)
    exchange = [remote(s, d.at[rows], w_send.at[i], w_recv.at[i], partner) for i, (s, d, rows) in enumerate(wide)]
    for copy in exchange:
        copy.start()

    theirs = pl.ds(pl.multiple_of((1 - c) * feat, feat), feat)
    theirs_rows = pl.ds(pl.multiple_of((1 - c) * (tile // 2), tile // 2), tile // 2)

    def have(i):
        rows = theirs_rows if i in (2, 3) else theirs
        local[3 + i].wait()
        arrived(wide[i][1].at[rows], w_recv.at[i])

    def tile_lanes(s):
        distance = jnp.where(near, NEAR[s], FAR[s])
        return pl.ds(pl.multiple_of(lax.rem(y + n_chip + distance, n_chip) * tile, tile), tile)

    for i in range(3):
        local[i].wait()
    have(1)
    for s in range(4):
        where = tile_lanes(s)
        grad, score, chosen = gg[:, where], sc[:, where], ids[:, where]
        total = jnp.sum(score, axis=0, keepdims=True)
        mixed = jnp.sum(grad * score, axis=0, keepdims=True)
        logit = 2.5 * (grad - mixed / total) / total * score * (1.0 - score)
        n_experts = wr.shape[1]
        rows = lax.broadcasted_iota(jnp.int32, (n_experts, tile), 0)
        dense = jnp.zeros((n_experts, tile), F32)
        for k in range(grad.shape[0]):
            dense = dense + jnp.where(chosen[k : k + 1] == rows, logit[k : k + 1], 0.0)
        rterm[s] = jnp.dot(wr[...], dense.astype(BF16), preferred_element_type=F32)

    have(2)
    have(3)

    @pl.when(near)
    def _():
        a, b = pa[...].astype(F32), pb[...].astype(F32)
        sigma = 1.0 / (1.0 + jnp.exp(-a))
        c1[...] = b * sigma * (1.0 + a * (1.0 - sigma))
        c2[...] = a * sigma

    have(0)

    width, gate_width = hid // PARTS, 2 * hid // PARTS

    def cut(k):
        return pl.ds(k * width, width)

    def wide_cut(k):
        return pl.ds(k * gate_width, gate_width)

    def rs_copy(src, slot, device, k):
        return remote(sbuf.at[src, :, cut(k)], rbuf.at[slot, :, cut(k)], rs_send.at[src, k], rs_recv.at[slot, k], device)

    def rs_arrived(slot, k):
        arrived(rbuf.at[slot, :, cut(k)], rs_recv.at[slot, k])

    def ag_copy(here, there, device, send, k):
        return remote(
            gbuf.at[here, :, wide_cut(k)], gbuf.at[there, :, wide_cut(k)], ag_send.at[send, k], ag_recv.at[there, k], device
        )

    def ag_arrived(slot, k):
        arrived(gbuf.at[slot, :, wide_cut(k)], ag_recv.at[slot, k])

    def step(s, k, slots):
        value = pf[:, cut(k)]
        for slot in slots:
            rs_arrived(slot, k)
            value = value + rbuf[slot, :, cut(k)].astype(F32)
        return value

    first, second = tuple(range(PARTS // 2)), tuple(range(PARTS // 2, PARTS))
    for s in range(4):
        for other in range(2):
            rows = pl.ds(other * feat, feat)
            arrived(up.at[s, rows], a_recv.at[s, other])
        pf[...] = lax.dot_general(up[s], dn[...], (((0,), (0,)), ((), ())), preferred_element_type=F32)

        @pl.when(near)
        def _(s=s):
            for k in range(PARTS):
                value = step(s, k, ((), (0,), (1,), (2, 3))[s])
                if s < 3:
                    sbuf[s, :, cut(k)] = value.astype(BF16)
                    if s == 0:
                        rs_copy(0, k // (PARTS // 2), (plus, minus)[k // (PARTS // 2)], k).start()
                    else:
                        rs_copy(s, s + 1, (plus, minus)[s - 1], k).start()
                else:
                    gbuf[3, :, cut(k)] = (value * c1[:, cut(k)]).astype(BF16)
                    gbuf[3, :, cut(PARTS + k)] = (value * c2[:, cut(k)]).astype(BF16)
                    if k % 2 == 1:
                        for j in (k // 2, PARTS // 2 + k // 2):
                            ag_copy(3, 3, plus, 0, j).start()
                            ag_copy(3, 2, minus, 1, j).start()

        @pl.when(far)
        def _(s=s):
            for k in second + first if s == 0 else first + second:
                summed = s >= 2 or k in (first, second)[s]
                sbuf[s, :, cut(k)] = step(s, k, (s,) if summed else ()).astype(BF16)
                rs_copy(s, s, (plus, minus)[s % 2], k).start()

    have(4)
    have(5)

    for s in (3, 2, 1, 0):

        @pl.when(near)
        def _(s=s):
            if s == 2:
                for k in LEAVING:
                    ag_arrived(2, k)
                    ag_copy(2, 1, plus, 2, k).start()
                    ag_arrived(1, k)
                    ag_copy(1, 0, minus, 3, k).start()
            if s == 0:
                for k in LEAVING:
                    ag_arrived(0, k)

        @pl.when(far)
        def _(s=s):
            if s == 3:
                for k in LEAVING:
                    ag_arrived(3, k)
                    ag_copy(3, 2, plus, 0, k).start()
                    ag_arrived(2, k)
                    ag_copy(2, 1, minus, 1, k).start()
            if s == 1:
                for k in LEAVING:
                    ag_arrived(1, k)
                    if k in first:
                        ag_copy(1, 0, plus, 2, k).start()
                    ag_arrived(0, k)
                    if k in second:
                        ag_copy(0, 0, minus, 3, k).start()

        nt = (((1,), (1,)), ((), ()))
        for other in range(2):
            rows = pl.ds(other * feat, feat)
            result = (
                lax.dot_general(wg[rows], gbuf[s, :, :hid], nt, preferred_element_type=F32)
                + lax.dot_general(wu[rows], gbuf[s, :, hid:], nt, preferred_element_type=F32)
                + rterm[s, rows]
            )
            obuf[s, rows] = result.astype(BF16)
            remote(
                obuf.at[s, rows], out_ref.at[:, tile_lanes(s)], d_send.at[s, other], d_recv.at[s, role],
                (before, 2 * y + other),
            ).start()

    for copy in incoming:
        copy.wait_send()
    for copy in exchange:
        copy.wait_send()

    def ag_sent(slot, send, k):
        sent(gbuf.at[slot, :, wide_cut(k)], ag_send.at[send, k])

    for k in range(PARTS):

        @pl.when(near)
        def _(k=k):
            for s in range(3):
                sent(sbuf.at[s, :, cut(k)], rs_send.at[s, k])
            for slot, send in ((3, 0), (3, 1), (2, 2), (1, 3)):
                ag_sent(slot, send, k)

        @pl.when(far)
        def _(k=k):
            for s in range(4):
                sent(sbuf.at[s, :, cut(k)], rs_send.at[s, k])
            ag_sent(3, 0, k)
            ag_sent(2, 1, k)
            if k in first:
                ag_sent(1, 2, k)
            else:
                ag_sent(0, 3, k)

    for s in range(4):
        for other in range(2):
            sent(obuf.at[s, pl.ds(other * feat, feat)], d_send.at[s, other])
            arrived(out_ref.at[:, pl.ds(0, tile)], d_recv.at[s, other])


def shards(upstream, shared_down, shared_gate, shared_up, router_weight, gate_pre, up_pre, gate_grad, gate_scores, expert_ids):
    n_pipe = lax.axis_size("pipe")
    n_chip = lax.axis_size("expert") // 2
    _, tokens, feat = upstream.shape
    rows, hid = gate_pre.shape[1:]
    tile = 2 * rows
    n_experts = router_weight.shape[2]
    top = gate_grad.shape[2]
    args = (
        upstream[0].T, shared_down[0].T, shared_gate[0], shared_up[0], router_weight[0], gate_pre[0], up_pre[0],
        gate_grad[0].T, gate_scores[0].T, expert_ids[0].T,
    )
    vm = pltpu.VMEM
    dma = pltpu.SemaphoreType.DMA
    out = pl.pallas_call(
        functools.partial(kernel, n_pipe, n_chip),
        out_shape=jax.ShapeDtypeStruct((feat, tokens), BF16),
        in_specs=[pl.BlockSpec(memory_space=pl.ANY)] * len(args),
        out_specs=pl.BlockSpec(memory_space=pl.ANY),
        scratch_shapes=[
            vm((4, 2 * feat, tile), BF16),
            vm((2 * feat, hid), BF16),
            vm((2 * feat, hid), BF16),
            vm((2 * feat, hid), BF16),
            vm((2 * feat, n_experts), BF16),
            vm((tile, hid), BF16),
            vm((tile, hid), BF16),
            vm((top, tokens), F32),
            vm((top, tokens), F32),
            vm((top, tokens), jnp.int32),
            vm((tile, hid), F32),
            vm((tile, hid), F32),
            vm((tile, hid), F32),
            vm((4, tile, hid), BF16),
            vm((4, tile, hid), BF16),
            vm((4, tile, 2 * hid), BF16),
            vm((4, 2 * feat, tile), F32),
            vm((4, 2 * feat, tile), BF16),
            dma((9,)), dma((8,)), dma((4, 2)), dma((6,)), dma((6,)),
            dma((4, PARTS)), dma((4, PARTS)), dma((4, PARTS)), dma((4, PARTS)), dma((4, 2)), dma((4, 2)),
        ],
        compiler_params=pltpu.CompilerParams(collective_id=0, has_side_effects=True, vmem_limit_bytes=67043328),
    )(*args)
    return out.T[None]


def solution(mesh):
    in_specs = (
        P("pipe", None, "expert"),
        P("pipe", None, "expert"),
        P("pipe", "expert", None),
        P("pipe", "expert", None),
        P("pipe", "expert", None),
        P("pipe", "expert", None),
        P("pipe", "expert", None),
        P("pipe", None, None),
        P("pipe", None, None),
        P("pipe", None, None),
    )
    out_specs = P("pipe", None, "expert")
    return jax.shard_map(shards, mesh=mesh, in_specs=in_specs, out_specs=out_specs, check_vma=False)
```

```python
import functools

import jax
import jax.numpy as jnp
from jax import lax
from jax.experimental import pallas as pl
from jax.experimental.pallas import tpu as pltpu
from jax.sharding import PartitionSpec as P

MESH = pl.DeviceIdType.MESH
F32 = jnp.float32
BF16 = jnp.bfloat16
NEAR = (4, 2, -2, 0)
FAR = (3, -3, 1, -1)
PARTS = 8
LEAVING = tuple(k for i in range(PARTS // 2) for k in (i, PARTS // 2 + i))


def kernel(
    n_pipe, n_chip,
    up_ref, dn_ref, wg_ref, wu_ref, wr_ref, pa_ref, pb_ref, gg_ref, sc_ref, id_ref,
    out_ref,
    up, dn, wg, wu, wr, pa, pb, gg, sc, ids, c1, c2, pf, rbuf, sbuf, gbuf, rterm, obuf,
    loc_sem, a_send, a_recv, w_send, w_recv, rs_send, rs_recv, ag_send, ag_recv, d_send, d_recv,
):
    feat = up_ref.shape[0]
    tile = pa_ref.shape[0] * 2
    hid = pa_ref.shape[1]
    p = lax.axis_index("pipe")
    e = lax.axis_index("expert")
    y, c = e // 2, e % 2
    role = lax.rem(c + y, 2)
    before = lax.rem(p + n_pipe - 1, n_pipe)
    after = lax.rem(p + 1, n_pipe)
    partner = (p, 2 * y + 1 - c)
    plus = (p, 2 * lax.rem(y + 1, n_chip) + c)
    minus = (p, 2 * lax.rem(y + n_chip - 1, n_chip) + c)
    near = role == 0
    far = role == 1

    def remote(src, dst, send, recv, device):
        return pltpu.make_async_remote_copy(
            src_ref=src, dst_ref=dst, send_sem=send, recv_sem=recv, device_id=device, device_id_type=MESH
        )

    def arrived(dst, recv):
        remote(dst, dst, recv, recv, partner).wait_recv()

    def sent(src, send):
        remote(src, src, send, send, partner).wait_send()

    barrier = pltpu.get_barrier_semaphore()
    for device in ((after, 2 * y), (after, 2 * y + 1), partner, plus, minus):
        pl.semaphore_signal(barrier, inc=1, device_id=device, device_id_type=MESH)

    mine = pl.ds(pl.multiple_of(c * feat, feat), feat)
    mine_rows = pl.ds(pl.multiple_of(c * (tile // 2), tile // 2), tile // 2)
    wide = ((dn_ref, dn, mine), (wr_ref, wr, mine), (pa_ref, pa, mine_rows), (pb_ref, pb, mine_rows),
            (wg_ref, wg, mine), (wu_ref, wu, mine))
    local = [pltpu.make_async_copy(s, d, loc_sem.at[i]) for i, (s, d) in enumerate(((gg_ref, gg), (sc_ref, sc), (id_ref, ids)))]
    local += [pltpu.make_async_copy(s, d.at[rows], loc_sem.at[3 + i]) for i, (s, d, rows) in enumerate(wide)]
    for copy in local:
        copy.start()

    pl.semaphore_wait(barrier, 5)

    def lanes(distance):
        return pl.ds(pl.multiple_of(lax.rem(y + n_chip + distance, n_chip) * tile, tile), tile)

    incoming = []
    for i in range(8):
        target, slot = i % 2, i // 2
        distance = jnp.where(lax.rem(target + y, 2) == 0, NEAR[slot], FAR[slot])
        copy = remote(
            up_ref.at[:, lanes(distance)], up.at[slot, mine], a_send.at[i], a_recv.at[slot, c], (before, 2 * y + target)
        )
        copy.start()
        incoming.append(copy)
    exchange = [remote(s, d.at[rows], w_send.at[i], w_recv.at[i], partner) for i, (s, d, rows) in enumerate(wide)]
    for copy in exchange[:4]:
        copy.start()

    theirs = pl.ds(pl.multiple_of((1 - c) * feat, feat), feat)
    theirs_rows = pl.ds(pl.multiple_of((1 - c) * (tile // 2), tile // 2), tile // 2)

    def have(i):
        rows = theirs_rows if i in (2, 3) else theirs
        local[3 + i].wait()
        arrived(wide[i][1].at[rows], w_recv.at[i])

    def tile_lanes(s):
        distance = jnp.where(near, NEAR[s], FAR[s])
        return pl.ds(pl.multiple_of(lax.rem(y + n_chip + distance, n_chip) * tile, tile), tile)

    def router_term():
        for i in range(3):
            local[i].wait()
        have(1)
        for s in range(4):
            where = tile_lanes(s)
            grad, score, chosen = gg[:, where], sc[:, where], ids[:, where]
            total = jnp.sum(score, axis=0, keepdims=True)
            mixed = jnp.sum(grad * score, axis=0, keepdims=True)
            logit = 2.5 * (grad - mixed / total) / total * score * (1.0 - score)
            n_experts = wr.shape[1]
            rows = lax.broadcasted_iota(jnp.int32, (n_experts, tile), 0)
            dense = jnp.zeros((n_experts, tile), F32)
            for k in range(grad.shape[0]):
                dense = dense + jnp.where(chosen[k : k + 1] == rows, logit[k : k + 1], 0.0)
            rterm[s] = jnp.dot(wr[...], dense.astype(BF16), preferred_element_type=F32)

    def coefficients():
        have(2)
        have(3)

        @pl.when(near)
        def _():
            a, b = pa[...].astype(F32), pb[...].astype(F32)
            sigma = 1.0 / (1.0 + jnp.exp(-a))
            c1[...] = b * sigma * (1.0 + a * (1.0 - sigma))
            c2[...] = a * sigma

    have(0)

    width, gate_width = hid // PARTS, 2 * hid // PARTS

    def cut(k):
        return pl.ds(k * width, width)

    def wide_cut(k):
        return pl.ds(k * gate_width, gate_width)

    def rs_copy(src, slot, device, k):
        return remote(sbuf.at[src, :, cut(k)], rbuf.at[slot, :, cut(k)], rs_send.at[src, k], rs_recv.at[slot, k], device)

    def rs_arrived(slot, k):
        arrived(rbuf.at[slot, :, cut(k)], rs_recv.at[slot, k])

    def ag_copy(here, there, device, send, k):
        return remote(
            gbuf.at[here, :, wide_cut(k)], gbuf.at[there, :, wide_cut(k)], ag_send.at[send, k], ag_recv.at[there, k], device
        )

    def ag_arrived(slot, k):
        arrived(gbuf.at[slot, :, wide_cut(k)], ag_recv.at[slot, k])

    def step(s, k, slots):
        value = pf[:, cut(k)]
        for slot in slots:
            rs_arrived(slot, k)
            value = value + rbuf[slot, :, cut(k)].astype(F32)
        return value

    first, second = tuple(range(PARTS // 2)), tuple(range(PARTS // 2, PARTS))
    for s in range(4):
        for other in range(2):
            rows = pl.ds(other * feat, feat)
            arrived(up.at[s, rows], a_recv.at[s, other])
        pf[...] = lax.dot_general(up[s], dn[...], (((0,), (0,)), ((), ())), preferred_element_type=F32)

        @pl.when(near)
        def _(s=s):
            for k in range(PARTS):
                value = step(s, k, ((), (0,), (1,), (2, 3))[s])
                if s < 3:
                    sbuf[s, :, cut(k)] = value.astype(BF16)
                    if s == 0:
                        rs_copy(0, k // (PARTS // 2), (plus, minus)[k // (PARTS // 2)], k).start()
                    else:
                        rs_copy(s, s + 1, (plus, minus)[s - 1], k).start()
                else:
                    gbuf[3, :, cut(k)] = (value * c1[:, cut(k)]).astype(BF16)
                    gbuf[3, :, cut(PARTS + k)] = (value * c2[:, cut(k)]).astype(BF16)
                    if k % 2 == 1:
                        for j in (k // 2, PARTS // 2 + k // 2):
                            ag_copy(3, 3, plus, 0, j).start()
                            ag_copy(3, 2, minus, 1, j).start()

        @pl.when(far)
        def _(s=s):
            for k in second + first if s == 0 else first + second:
                summed = s >= 2 or k in (first, second)[s]
                sbuf[s, :, cut(k)] = step(s, k, (s,) if summed else ()).astype(BF16)
                rs_copy(s, s, (plus, minus)[s % 2], k).start()

        if s == 0:
            for copy in exchange[4:]:
                copy.start()
            router_term()
        if s == 1:
            coefficients()

    have(4)
    have(5)

    for s in (3, 2, 1, 0):

        @pl.when(near)
        def _(s=s):
            if s == 2:
                for k in LEAVING:
                    ag_arrived(2, k)
                    ag_copy(2, 1, plus, 2, k).start()
                    ag_arrived(1, k)
                    ag_copy(1, 0, minus, 3, k).start()
            if s == 0:
                for k in LEAVING:
                    ag_arrived(0, k)

        @pl.when(far)
        def _(s=s):
            if s == 3:
                for k in LEAVING:
                    ag_arrived(3, k)
                    ag_copy(3, 2, plus, 0, k).start()
                    ag_arrived(2, k)
                    ag_copy(2, 1, minus, 1, k).start()
            if s == 1:
                for k in LEAVING:
                    ag_arrived(1, k)
                    if k in first:
                        ag_copy(1, 0, plus, 2, k).start()
                    ag_arrived(0, k)
                    if k in second:
                        ag_copy(0, 0, minus, 3, k).start()

        nt = (((1,), (1,)), ((), ()))
        for other in range(2):
            rows = pl.ds(other * feat, feat)
            result = (
                lax.dot_general(wg[rows], gbuf[s, :, :hid], nt, preferred_element_type=F32)
                + lax.dot_general(wu[rows], gbuf[s, :, hid:], nt, preferred_element_type=F32)
                + rterm[s, rows]
            )
            obuf[s, rows] = result.astype(BF16)
            remote(
                obuf.at[s, rows], out_ref.at[:, tile_lanes(s)], d_send.at[s, other], d_recv.at[s, role],
                (before, 2 * y + other),
            ).start()

    for copy in incoming:
        copy.wait_send()
    for copy in exchange:
        copy.wait_send()

    def ag_sent(slot, send, k):
        sent(gbuf.at[slot, :, wide_cut(k)], ag_send.at[send, k])

    for k in range(PARTS):

        @pl.when(near)
        def _(k=k):
            for s in range(3):
                sent(sbuf.at[s, :, cut(k)], rs_send.at[s, k])
            for slot, send in ((3, 0), (3, 1), (2, 2), (1, 3)):
                ag_sent(slot, send, k)

        @pl.when(far)
        def _(k=k):
            for s in range(4):
                sent(sbuf.at[s, :, cut(k)], rs_send.at[s, k])
            ag_sent(3, 0, k)
            ag_sent(2, 1, k)
            if k in first:
                ag_sent(1, 2, k)
            else:
                ag_sent(0, 3, k)

    for s in range(4):
        for other in range(2):
            sent(obuf.at[s, pl.ds(other * feat, feat)], d_send.at[s, other])
            arrived(out_ref.at[:, pl.ds(0, tile)], d_recv.at[s, other])


def shards(upstream, shared_down, shared_gate, shared_up, router_weight, gate_pre, up_pre, gate_grad, gate_scores, expert_ids):
    n_pipe = lax.axis_size("pipe")
    n_chip = lax.axis_size("expert") // 2
    _, tokens, feat = upstream.shape
    rows, hid = gate_pre.shape[1:]
    tile = 2 * rows
    n_experts = router_weight.shape[2]
    top = gate_grad.shape[2]
    args = (
        upstream[0].T, shared_down[0].T, shared_gate[0], shared_up[0], router_weight[0], gate_pre[0], up_pre[0],
        gate_grad[0].T, gate_scores[0].T, expert_ids[0].T,
    )
    vm = pltpu.VMEM
    dma = pltpu.SemaphoreType.DMA
    out = pl.pallas_call(
        functools.partial(kernel, n_pipe, n_chip),
        out_shape=jax.ShapeDtypeStruct((feat, tokens), BF16),
        in_specs=[pl.BlockSpec(memory_space=pl.ANY)] * len(args),
        out_specs=pl.BlockSpec(memory_space=pl.ANY),
        scratch_shapes=[
            vm((4, 2 * feat, tile), BF16),
            vm((2 * feat, hid), BF16),
            vm((2 * feat, hid), BF16),
            vm((2 * feat, hid), BF16),
            vm((2 * feat, n_experts), BF16),
            vm((tile, hid), BF16),
            vm((tile, hid), BF16),
            vm((top, tokens), F32),
            vm((top, tokens), F32),
            vm((top, tokens), jnp.int32),
            vm((tile, hid), F32),
            vm((tile, hid), F32),
            vm((tile, hid), F32),
            vm((4, tile, hid), BF16),
            vm((4, tile, hid), BF16),
            vm((4, tile, 2 * hid), BF16),
            vm((4, 2 * feat, tile), F32),
            vm((4, 2 * feat, tile), BF16),
            dma((9,)), dma((8,)), dma((4, 2)), dma((6,)), dma((6,)),
            dma((4, PARTS)), dma((4, PARTS)), dma((4, PARTS)), dma((4, PARTS)), dma((4, 2)), dma((4, 2)),
        ],
        compiler_params=pltpu.CompilerParams(collective_id=0, has_side_effects=True, vmem_limit_bytes=67043328),
    )(*args)
    return out.T[None]


def solution(mesh):
    in_specs = (
        P("pipe", None, "expert"),
        P("pipe", None, "expert"),
        P("pipe", "expert", None),
        P("pipe", "expert", None),
        P("pipe", "expert", None),
        P("pipe", "expert", None),
        P("pipe", "expert", None),
        P("pipe", None, None),
        P("pipe", None, None),
        P("pipe", None, None),
    )
    out_specs = P("pipe", None, "expert")
    return jax.shard_map(shards, mesh=mesh, in_specs=in_specs, out_specs=out_specs, check_vma=False)
```
